32 devices in a mesh: freq: 2 (over x), trial: 16 (over z, y, core).
Axes of the slice: x: 2, y: 2, z: 4, core: 2. Of those that a mesh axis runs over, the one named last changes fastest.
Arguments:
- signals: bfloat16 [32, 306, 1024], P('trial'), may hold values from -6 to 6
- kernel: bfloat16 [8192, 306], P('trial'), may hold values from -0.3125 to 0.3125
- freqs: float32 [10], P('freq'), may hold values from 3.6 to 66
Outputs:
- rel_power: float32 [8192, 160], P('trial', 'freq')
- itc_score: float32 [8192, 160], P('trial', 'freq')
The draws below stay inside these ranges and needn't reach their ends.
All inputs are finite; a program needn't handle non-finite values.
Results may differ from the reference program's by a relative error of at most 0.0003.
Values may be sent and summed in bfloat16 or wider, within the bound.
A program may use at most 64 MiB of HBM per device.

```python
import jax
import jax.numpy as jnp
from jax import lax

C = 306
SRC = 8192
SAMPLES = 1024
TOUT = 16
FREQS = 10
TRIALS = 32


def draw_freqs(key, part):
    ladder = jnp.arange(FREQS, dtype=jnp.float32) / max(FREQS - 1, 1)
    base = 4.0 * jnp.exp(ladder * jnp.log(15.0))
    jitter = jax.random.uniform(key, (FREQS,), jnp.float32, 0.97, 1.03)
    values = base * jitter
    return jax.random.permutation(jax.random.fold_in(key, 7), values).astype(jnp.float32)


def level_of(stream_key, dims, shards, low, top_value):
    def one(axis_at, shards_of):
        draws = jax.random.uniform(jax.random.fold_in(jax.random.fold_in(stream_key, 6), axis_at), (shards_of,), jnp.float32, low / len(shards), top_value / len(shards))
        return jnp.repeat(jnp.exp(draws), dims[axis_at] // shards_of).reshape((-1,) + (1,) * (len(dims) - axis_at - 1))

    level = one(*shards[0])
    for cut in shards[1:]:
        level = level * one(*cut)
    return level


def gaussian(stream_key, shape, width, bound, cuts=(), kind=jnp.bfloat16):
    array = width * jax.random.normal(stream_key, shape, jnp.float32)
    if cuts:
        array = array * level_of(stream_key, shape, cuts, -0.22, 0.18)
    return jnp.clip(array, -bound, bound).astype(kind)


def setup_inputs(seed: int = 0) -> dict:
    streams_of = jax.random.split(jax.random.key(seed), 4)
    return {
        "signals": gaussian(streams_of[0], (TRIALS, C, SAMPLES), 1.0, 6.0, ((0, 16),)),
        "kernel": gaussian(streams_of[1], (SRC, C), C ** -0.5, 0.3125, ((0, 16),)),
        "freqs": draw_freqs(jax.random.fold_in(streams_of[3], 71), 0),
    }


CYCLES = 7.0
SAMPLE_RATE = 1000.0
PHASE_FLOOR = 0.25
MEAN_EPSILON = 1e-06

def wavelet_table(frequencies, sample_count, point_count):
    stride = sample_count // point_count
    moments = jnp.arange(sample_count, dtype=frequencies.dtype)[:, None, None]
    centres = (jnp.arange(point_count, dtype=frequencies.dtype) * stride + stride // 2)[None, None, :]
    widths = CYCLES * SAMPLE_RATE / (2.0 * jnp.pi) / frequencies[None, :, None]
    offset = moments - centres
    envelope = jnp.exp(-offset * offset / (2.0 * widths * widths)) * (8.0 / widths)
    angles = 2.0 * jnp.pi / SAMPLE_RATE * frequencies[None, :, None] * offset
    stacked = jnp.stack([envelope * jnp.cos(angles), envelope * jnp.sin(angles)], axis=1)
    return stacked.reshape(sample_count, -1)

def reference(signals, kernel, freqs):
    trial_count, chan_count, sample_count = signals.shape
    table = wavelet_table(freqs, sample_count, TOUT)
    flat = signals.reshape(trial_count * chan_count, sample_count).astype(jnp.float32)
    coefficients = jnp.dot(flat, table, precision=lax.Precision.HIGHEST, preferred_element_type=jnp.float32)
    coefficients = coefficients.reshape(trial_count, chan_count, -1)
    span = FREQS * TOUT
    kernel_wide = kernel.astype(jnp.float32)

    def one_trial(carry, block):
        source = jnp.dot(kernel_wide, block, precision=lax.Precision.HIGHEST)
        real_part = source[:, :span]
        imag_part = source[:, span:]
        magnitude = real_part * real_part + imag_part * imag_part
        inverse = lax.rsqrt(magnitude + PHASE_FLOOR)
        return ((carry[0] + magnitude, carry[1] + real_part * inverse, carry[2] + imag_part * inverse), None)
    zeros_init = jnp.zeros((SRC, span), jnp.float32)
    sums, unused = lax.scan(one_trial, (zeros_init, zeros_init, zeros_init), coefficients)
    power = sums[0] / TRIALS
    mean_power = lax.optimization_barrier(jnp.sum(power, axis=1, keepdims=True)) / (FREQS * TOUT)
    rel_power = power / (mean_power + MEAN_EPSILON)
    itc_score = (sums[1] * sums[1] + sums[2] * sums[2]) / TRIALS
    return (rel_power, itc_score)
```

```python
import functools
import math

import jax
import jax.numpy as jnp
from jax import lax
from jax.experimental import pallas as pl
from jax.experimental.pallas import tpu as pltpu
from jax.sharding import PartitionSpec as P

TOUT = 16
CYCLES = 7.0
SAMPLE_RATE = 1000.0
PHASE_FLOOR = 0.25
MEAN_EPSILON = 1e-06
LANES = 128
MESH = pl.DeviceIdType.MESH
F32 = jnp.float32
BF16 = jnp.bfloat16


def grid_of(chips):
    outer = 1
    while outer * outer < chips or chips % outer:
        outer += 1
    return outer, chips // outer


def polynomial(x2, terms):
    total = jnp.full_like(x2, terms[-1])
    for term in reversed(terms[:-1]):
        total = total * x2 + term
    return total


SIN_TERMS = [(-1) ** i * math.pi ** (2 * i + 1) / math.factorial(2 * i + 1) for i in range(8)]
COS_TERMS = [(-1) ** i * math.pi ** (2 * i) / math.factorial(2 * i) for i in range(8)]


def wavelet_rows(freq, points, samples):
    stride = samples // points
    moments = lax.broadcasted_iota(jnp.int32, (points, samples), 1)
    centres = lax.broadcasted_iota(jnp.int32, (points, samples), 0) * stride + stride // 2
    scaled = (moments - centres).astype(F32) * freq
    rate = 2.0 * math.pi / (CYCLES * SAMPLE_RATE)
    envelope = jnp.exp(scaled * scaled * (-0.5 * rate * rate)) * (freq * (8.0 * rate))
    turns = scaled * (1.0 / SAMPLE_RATE)
    part = turns - jnp.floor(turns + 0.5)
    square = part * part
    half_sin = part * polynomial(square, SIN_TERMS)
    half_cos = polynomial(square, COS_TERMS)
    return (
        envelope * (1.0 - 2.0 * half_sin * half_sin),
        envelope * (2.0 * half_sin * half_cos),
    )


def split(x):
    high = x.astype(BF16)
    return high, (x - high.astype(F32)).astype(BF16)


def encode(rows):
    return split(rows)


def decode(block):
    return block[0], block[1]


def body(
    outer,
    inner,
    groups,
    freqs_ref,
    signals_ref,
    kernel_ref,
    rel_ref,
    itc_ref,
    table,
    rest_rows,
    blocks,
    peer_kernel,
    rest_pad,
    weights,
    acc,
    peer_acc,
    sums,
    out_sums,
    recv,
    outer_send,
    inner_send,
    pair_send,
    pair_recv,
    sum_send,
    sum_recv,
):
    local, chans, samples = signals_ref.shape
    sources = kernel_ref.shape[0]
    bands = freqs_ref.shape[0]
    span = bands * TOUT
    main = chans // LANES * LANES
    rest = chans - main
    slot_rows = LANES // local
    chunks = blocks.shape[1]

    group = lax.axis_index("freq")
    place = lax.axis_index("trial")
    core = place % 2
    chip = place // 2
    a = chip // inner
    b = chip % inner
    partner = place + 1 - 2 * core

    def at(oa, ob):
        return (oa * inner + ob) * 2 + core

    barrier = pltpu.get_barrier_semaphore()

    def greet(target):
        pl.semaphore_signal(barrier, inc=1, device_id=target, device_id_type=MESH)

    for ahead in (-1, 1):
        ia = a + ahead
        ib = b + ahead

        @pl.when((ia >= 0) & (ia < outer))
        def _():
            greet({"trial": at(ia, b)})

        @pl.when((ib >= 0) & (ib < inner))
        def _():
            greet({"trial": at(a, ib)})

    others = []
    for step in range(groups):
        for flip in range(2):
            if step or flip:
                others.append((step, flip))

    def other(step, flip):
        there = (group + step) % groups
        seat = partner if flip else place
        return {"freq": there, "trial": seat}

    for step, flip in others:
        greet(other(step, flip))
    near = (
        jnp.minimum(a, 1)
        + jnp.minimum(outer - 1 - a, 1)
        + jnp.minimum(b, 1)
        + jnp.minimum(inner - 1 - b, 1)
    )
    pl.semaphore_wait(barrier, near + len(others))

    kernel_copy = pltpu.make_async_remote_copy(
        src_ref=kernel_ref,
        dst_ref=peer_kernel,
        send_sem=pair_send.at[0],
        recv_sem=pair_recv.at[0],
        device_id={"trial": partner},
        device_id_type=MESH,
    )
    kernel_copy.start()

    for band in range(bands):
        cos_rows, sin_rows = wavelet_rows(freqs_ref[band], TOUT, samples)
        for half, rows in enumerate((cos_rows, sin_rows)):
            high, low = split(rows)
            first = half * span + band * TOUT
            table[first : first + TOUT, :] = high
            table[2 * span + first : 2 * span + first + TOUT, :] = low
    rest_rows[...] = jnp.zeros_like(rest_rows)
    for j in range(local):
        rest_rows[j * slot_rows : j * slot_rows + rest, :] = signals_ref[j, main:chans, :]

    mine = a * inner + b
    pieces = [(j * main, main, functools.partial(lambda j: signals_ref[j, 0:main, :], j)) for j in range(local)]
    pieces.append((local * main, LANES, lambda: rest_rows[...]))
    for start, width, load in pieces:
        both = lax.dot_general(
            table[...], load(), (((1,), (1,)), ((), ())), preferred_element_type=F32
        )
        coded = encode(both[: 2 * span] + both[2 * span :])
        for chunk in range(chunks):
            blocks[mine, chunk, :, start : start + width] = coded[chunk]

    def outer_copy(oa, chunk, ahead):
        slot = oa * inner + b
        side = (ahead + 1) // 2
        return pltpu.make_async_remote_copy(
            src_ref=blocks.at[slot, chunk],
            dst_ref=blocks.at[slot, chunk],
            send_sem=outer_send.at[side, oa, chunk],
            recv_sem=recv.at[slot, chunk],
            device_id={"trial": at(a + ahead, b)},
            device_id_type=MESH,
        )

    def inner_copy(oa, ob, chunk, ahead):
        slot = oa * inner + ob
        side = (ahead + 1) // 2
        return pltpu.make_async_remote_copy(
            src_ref=blocks.at[slot, chunk],
            dst_ref=blocks.at[slot, chunk],
            send_sem=inner_send.at[side, slot, chunk],
            recv_sem=recv.at[slot, chunk],
            device_id={"trial": at(a, b + ahead)},
            device_id_type=MESH,
        )

    def outer_sends(oa, chunk, act):
        @pl.when((oa <= a) & (a + 1 < outer))
        def _():
            act(outer_copy(oa, chunk, 1))

        @pl.when((oa >= a) & (a >= 1))
        def _():
            act(outer_copy(oa, chunk, -1))

    def inner_sends(oa, ob, chunk, act):
        @pl.when((ob <= b) & (b + 1 < inner))
        def _():
            act(inner_copy(oa, ob, chunk, 1))

        @pl.when((ob >= b) & (b >= 1))
        def _():
            act(inner_copy(oa, ob, chunk, -1))

    def start(copy):
        copy.start()

    def finish(copy):
        copy.wait_send()

    def nearest(k, here, count):
        left = here
        right = count - 1 - here
        both = 2 * jnp.minimum(left, right)
        dist = jnp.where(k <= both, (k + 1) // 2, k - both // 2)
        to_left = jnp.where(k <= both, k % 2, jnp.where(left > right, 1, 0))
        return here + dist - 2 * dist * to_left

    for chunk in range(chunks):
        outer_sends(a, chunk, start)
        inner_sends(a, b, chunk, start)

    acc[...] = jnp.zeros_like(acc)

    def place_weights(ref, first):
        wide = ref[:, 0:main].astype(F32).T.astype(BF16)
        rest_pad[...] = jnp.zeros_like(rest_pad)
        rest_pad[:, 0:rest] = ref[:, main:chans].astype(F32)
        tail = rest_pad[...].T.astype(BF16)[0:slot_rows]
        cols = slice(first, first + sources)
        for j in range(local):
            for copy in range(2):
                weights[j, copy * main : (copy + 1) * main, cols] = wide
                base = 2 * main + copy * LANES
                for other_slot in range(local):
                    rows = slice(base + other_slot * slot_rows, base + (other_slot + 1) * slot_rows)
                    weights[j, rows, cols] = tail if other_slot == j else jnp.zeros_like(tail)

    place_weights(kernel_ref, 0)
    kernel_copy.wait()
    place_weights(peer_kernel, sources)

    step_lanes = min(256, sources)
    tiles = sources // step_lanes

    def compute(slot):
        high, low = decode([blocks[slot, chunk] for chunk in range(chunks)])
        tail = local * main
        for j in range(local):
            left = jnp.concatenate(
                [
                    high[:, j * main : (j + 1) * main],
                    low[:, j * main : (j + 1) * main],
                    high[:, tail : tail + LANES],
                    low[:, tail : tail + LANES],
                ],
                axis=1,
            )
            for half in range(2):
                for tile in range(tiles):
                    lanes = slice(tile * step_lanes, (tile + 1) * step_lanes)
                    first = half * sources + tile * step_lanes
                    source = jnp.dot(
                        left,
                        weights[j, :, first : first + step_lanes],
                        preferred_element_type=F32,
                    )
                    real = source[:span]
                    imag = source[span:]
                    magnitude = real * real + imag * imag
                    inverse = lax.rsqrt(magnitude + PHASE_FLOOR)
                    acc[half, 0, :, lanes] += magnitude
                    acc[half, 1, :, lanes] += real * inverse
                    acc[half, 2, :, lanes] += imag * inverse

    def arrived(slot, chunk):
        pltpu.make_async_remote_copy(
            src_ref=blocks.at[slot, chunk],
            dst_ref=blocks.at[slot, chunk],
            send_sem=pair_send.at[0],
            recv_sem=recv.at[slot, chunk],
            device_id={"trial": partner},
            device_id_type=MESH,
        ).wait_recv()

    def event(e, carry):
        ka = e // inner
        kb = e % inner
        oa = nearest(ka, a, outer)
        ob = nearest(kb, b, inner)

        @pl.when(kb > 0)
        def _():
            for chunk in range(chunks):
                arrived(oa * inner + ob, chunk)
                inner_sends(oa, ob, chunk, start)

        compute(oa * inner + ob)

        @pl.when((kb == 0) & (ka + 1 < outer))
        def _():
            na = nearest(ka + 1, a, outer)
            for chunk in range(chunks):
                arrived(na * inner + b, chunk)
                outer_sends(na, chunk, start)
                inner_sends(na, b, chunk, start)

        return carry

    lax.fori_loop(0, outer * inner, event, 0)

    pair_copy = pltpu.make_async_remote_copy(
        src_ref=acc.at[1],
        dst_ref=peer_acc,
        send_sem=pair_send.at[1],
        recv_sem=pair_recv.at[1],
        device_id={"trial": partner},
        device_id_type=MESH,
    )
    pair_copy.start()
    for half in range(2):
        total = acc[half, 0, 0:8, :]
        for row in range(8, span, 8):
            total = total + acc[half, 0, row : row + 8, :]
        out_sums[half] = total
    sum_copies = []
    for index, (step, flip) in enumerate(others):
        slot = step * 2 + flip
        sum_copies.append(
            pltpu.make_async_remote_copy(
                src_ref=out_sums.at[flip],
                dst_ref=sums.at[slot - 1],
                send_sem=sum_send.at[index],
                recv_sem=sum_recv.at[index],
                device_id=other(step, flip),
                device_id_type=MESH,
            )
        )
    for copy in sum_copies:
        copy.start()

    trials = outer * inner * 2 * local
    pair_copy.wait()
    real = acc[0, 1] + peer_acc[1]
    imag = acc[0, 2] + peer_acc[2]
    itc_ref[...] = (real * real + imag * imag) / trials
    power = (acc[0, 0] + peer_acc[0]) / trials
    total = out_sums[0]
    for index, copy in enumerate(sum_copies):
        copy.wait()
        total = total + sums[index]
    mean_power = jnp.sum(total, axis=0, keepdims=True) / trials / (span * groups)
    rel_ref[...] = power / (mean_power + MEAN_EPSILON)

    def drain(e, carry):
        oa = e // inner
        ob = e % inner
        for chunk in range(chunks):
            inner_sends(oa, ob, chunk, finish)

            @pl.when(ob == b)
            def _():
                outer_sends(oa, chunk, finish)

        return carry

    lax.fori_loop(0, outer * inner, drain, 0)


def shards(signals, kernel, freqs):
    local, chans, samples = signals.shape
    sources = kernel.shape[0]
    span = freqs.shape[0] * TOUT
    groups = lax.axis_size("freq")
    chips = lax.axis_size("trial") // 2
    outer, inner = grid_of(chips)
    main = chans // LANES * LANES
    width = local * main + LANES
    depth = 2 * (main + LANES)
    chunks = 2
    vmem = pl.BlockSpec(memory_space=pltpu.VMEM)
    out = jax.ShapeDtypeStruct((span, sources), F32)
    dma = pltpu.SemaphoreType.DMA
    rel_power, itc_score = pl.pallas_call(
        functools.partial(body, outer, inner, groups),
        out_shape=(out, out),
        in_specs=[pl.BlockSpec(memory_space=pltpu.SMEM), vmem, vmem],
        out_specs=(vmem, vmem),
        scratch_shapes=[
            pltpu.VMEM((4 * span, samples), BF16),
            pltpu.VMEM((LANES, samples), BF16),
            pltpu.VMEM((chips, chunks, 2 * span, width), BF16),
            pltpu.VMEM((sources, chans), BF16),
            pltpu.VMEM((sources, LANES), F32),
            pltpu.VMEM((local, depth, 2 * sources), BF16),
            pltpu.VMEM((2, 3, span, sources), F32),
            pltpu.VMEM((3, span, sources), F32),
            pltpu.VMEM((2 * groups - 1, 8, sources), F32),
            pltpu.VMEM((2, 8, sources), F32),
            dma((chips, chunks)),
            dma((2, outer, chunks)),
            dma((2, chips, chunks)),
            dma((2,)),
            dma((2,)),
            dma((2 * groups - 1,)),
            dma((2 * groups - 1,)),
        ],
        compiler_params=pltpu.CompilerParams(collective_id=0, has_side_effects=True),
    )(freqs, signals, kernel)
    return rel_power.T, itc_score.T


def solution(mesh):
    return jax.shard_map(
        shards,
        mesh=mesh,
        in_specs=(P("trial", None, None), P("trial", None), P("freq")),
        out_specs=(P("trial", "freq"), P("trial", "freq")),
        check_vma=False,
    )
```

```python
import functools
import math

import jax
import jax.numpy as jnp
from jax import lax
from jax.experimental import pallas as pl
from jax.experimental.pallas import tpu as pltpu
from jax.sharding import PartitionSpec as P

TOUT = 16
CYCLES = 7.0
SAMPLE_RATE = 1000.0
PHASE_FLOOR = 0.25
MEAN_EPSILON = 1e-06
LANES = 128
MESH = pl.DeviceIdType.MESH
F32 = jnp.float32
BF16 = jnp.bfloat16


def grid_of(chips):
    outer = 1
    while outer * outer < chips or chips % outer:
        outer += 1
    return outer, chips // outer


def polynomial(x2, terms):
    total = jnp.full_like(x2, terms[-1])
    for term in reversed(terms[:-1]):
        total = total * x2 + term
    return total


SIN_TERMS = [(-1) ** i * math.pi ** (2 * i + 1) / math.factorial(2 * i + 1) for i in range(8)]
COS_TERMS = [(-1) ** i * math.pi ** (2 * i) / math.factorial(2 * i) for i in range(8)]


def wavelet_rows(freq, points, samples):
    stride = samples // points
    moments = lax.broadcasted_iota(jnp.int32, (points, samples), 1)
    centres = lax.broadcasted_iota(jnp.int32, (points, samples), 0) * stride + stride // 2
    scaled = (moments - centres).astype(F32) * freq
    rate = 2.0 * math.pi / (CYCLES * SAMPLE_RATE)
    envelope = jnp.exp(scaled * scaled * (-0.5 * rate * rate)) * (freq * (8.0 * rate))
    turns = scaled * (1.0 / SAMPLE_RATE)
    part = turns - jnp.floor(turns + 0.5)
    square = part * part
    half_sin = part * polynomial(square, SIN_TERMS)
    half_cos = polynomial(square, COS_TERMS)
    return (
        envelope * (1.0 - 2.0 * half_sin * half_sin),
        envelope * (2.0 * half_sin * half_cos),
    )


def split(x):
    high = x.astype(BF16)
    return high, (x - high.astype(F32)).astype(BF16)


POWER_LOG = 4
CODE_TOP = 2.0 ** (125.0 / 2**POWER_LOG)


def encode(rows, inverse):
    x = rows * inverse
    y = x * x
    for _ in range(POWER_LOG - 1):
        y = y * y
    return jnp.where(x < 0, -y, y).astype(BF16)


def decode(code, scale):
    y = code.astype(F32)
    size = jnp.maximum(jnp.abs(y), 1.2e-38)
    x = jnp.exp(jnp.log(size) * (1.0 / 2**POWER_LOG)) * scale
    return jnp.where(y < 0, -x, jnp.where(y > 0, x, 0.0))


def body(
    outer,
    inner,
    groups,
    freqs_ref,
    signals_ref,
    kernel_ref,
    rel_ref,
    itc_ref,
    mean_ref,
    table,
    plain,
    rest_rows,
    blocks,
    peer_kernel,
    rest_pad,
    weights,
    acc,
    peer_acc,
    sums,
    out_sums,
    recv,
    outer_send,
    inner_send,
    pair_send,
    pair_recv,
    sum_send,
    sum_recv,
):
    local, chans, samples = signals_ref.shape
    sources = kernel_ref.shape[1]
    bands = freqs_ref.shape[0]
    span = bands * TOUT
    main = chans // LANES * LANES
    rest = chans - main
    slot_rows = LANES // local
    chunks = blocks.shape[1]

    group = lax.axis_index("freq")
    place = lax.axis_index("trial")
    core = place % 2
    chip = place // 2
    a = chip // inner
    b = chip % inner
    partner = place + 1 - 2 * core

    def at(oa, ob):
        return (oa * inner + ob) * 2 + core

    barrier = pltpu.get_barrier_semaphore()

    def greet(target):
        pl.semaphore_signal(barrier, inc=1, device_id=target, device_id_type=MESH)

    for ahead in (-1, 1):
        ia = a + ahead
        ib = b + ahead

        @pl.when((ia >= 0) & (ia < outer))
        def _():
            greet({"trial": at(ia, b)})

        @pl.when((ib >= 0) & (ib < inner))
        def _():
            greet({"trial": at(a, ib)})

    others = []
    for step in range(groups):
        for flip in range(2):
            if step or flip:
                others.append((step, flip))

    def other(step, flip):
        there = (group + step) % groups
        seat = partner if flip else place
        return {"freq": there, "trial": seat}

    for step, flip in others:
        greet(other(step, flip))
    near = (
        jnp.minimum(a, 1)
        + jnp.minimum(outer - 1 - a, 1)
        + jnp.minimum(b, 1)
        + jnp.minimum(inner - 1 - b, 1)
    )
    pl.semaphore_wait(barrier, near + len(others))

    kernel_copy = pltpu.make_async_remote_copy(
        src_ref=kernel_ref,
        dst_ref=peer_kernel,
        send_sem=pair_send.at[0],
        recv_sem=pair_recv.at[0],
        device_id={"trial": partner},
        device_id_type=MESH,
    )
    kernel_copy.start()

    for band in range(bands):
        cos_rows, sin_rows = wavelet_rows(freqs_ref[band], TOUT, samples)
        for half, rows in enumerate((cos_rows, sin_rows)):
            high, low = split(rows)
            first = half * span + band * TOUT
            table[first : first + TOUT, :] = high
            table[2 * span + first : 2 * span + first + TOUT, :] = low
    rest_rows[...] = jnp.zeros_like(rest_rows)
    for j in range(local):
        rest_rows[j * slot_rows : j * slot_rows + rest, :] = signals_ref[j, main:chans, :]

    mine = a * inner + b
    pieces = [(j * main, main, functools.partial(lambda j: signals_ref[j, 0:main, :], j)) for j in range(local)]
    pieces.append((local * main, LANES, lambda: rest_rows[...]))
    top = jnp.zeros((2 * span, 1), F32)
    for start, width, load in pieces:
        both = lax.dot_general(
            table[...], load(), (((1,), (1,)), ((), ())), preferred_element_type=F32
        )
        value = both[: 2 * span] + both[2 * span :]
        plain[:, start : start + width] = value
        top = jnp.maximum(top, jnp.max(jnp.abs(value), axis=1, keepdims=True))
    scale = jnp.maximum(top * 1.01, 1e-30).astype(BF16)
    inverse = CODE_TOP / scale.astype(F32)
    lane = lax.broadcasted_iota(jnp.int32, (span, LANES), 1)
    for chunk in range(chunks):
        rows = slice(chunk * span, (chunk + 1) * span)
        for start, width, _ in pieces:
            coded = encode(plain[rows, start : start + width], inverse[rows])
            if start == local * main:
                coded = jnp.where(lane == rest, scale[rows].astype(F32), coded.astype(F32)).astype(BF16)
            blocks[mine, chunk, :, start : start + width] = coded

    def outer_copy(oa, chunk, ahead):
        slot = oa * inner + b
        side = (ahead + 1) // 2
        return pltpu.make_async_remote_copy(
            src_ref=blocks.at[slot, chunk],
            dst_ref=blocks.at[slot, chunk],
            send_sem=outer_send.at[side, oa, chunk],
            recv_sem=recv.at[slot, chunk],
            device_id={"trial": at(a + ahead, b)},
            device_id_type=MESH,
        )

    def inner_copy(oa, ob, chunk, ahead):
        slot = oa * inner + ob
        side = (ahead + 1) // 2
        return pltpu.make_async_remote_copy(
            src_ref=blocks.at[slot, chunk],
            dst_ref=blocks.at[slot, chunk],
            send_sem=inner_send.at[side, slot, chunk],
            recv_sem=recv.at[slot, chunk],
            device_id={"trial": at(a, b + ahead)},
            device_id_type=MESH,
        )

    def outer_sends(oa, chunk, act):
        @pl.when((oa <= a) & (a + 1 < outer))
        def _():
            act(outer_copy(oa, chunk, 1))

        @pl.when((oa >= a) & (a >= 1))
        def _():
            act(outer_copy(oa, chunk, -1))

    def inner_sends(oa, ob, chunk, act):
        @pl.when((ob <= b) & (b + 1 < inner))
        def _():
            act(inner_copy(oa, ob, chunk, 1))

        @pl.when((ob >= b) & (b >= 1))
        def _():
            act(inner_copy(oa, ob, chunk, -1))

    def start(copy):
        copy.start()

    def finish(copy):
        copy.wait_send()

    def nearest(k, here, count):
        left = here
        right = count - 1 - here
        both = 2 * jnp.minimum(left, right)
        dist = jnp.where(k <= both, (k + 1) // 2, k - both // 2)
        to_left = jnp.where(k <= both, k % 2, jnp.where(left > right, 1, 0))
        return here + dist - 2 * dist * to_left

    for chunk in range(chunks):
        outer_sends(a, chunk, start)
        inner_sends(a, b, chunk, start)

    acc[...] = jnp.zeros_like(acc)

    def place_weights(ref, first):
        wide = ref[0:main, :]
        rest_pad[...] = jnp.zeros_like(rest_pad)
        rest_pad[0:rest, :] = ref[main:chans, :]
        tail = rest_pad[...]
        cols = slice(first, first + sources)
        for j in range(local):
            for copy in range(2):
                weights[j, copy * main : (copy + 1) * main, cols] = wide
                base = 2 * main + copy * LANES
                for other_slot in range(local):
                    rows = slice(base + other_slot * slot_rows, base + (other_slot + 1) * slot_rows)
                    weights[j, rows, cols] = tail if other_slot == j else jnp.zeros_like(tail)

    place_weights(kernel_ref, 0)
    kernel_copy.wait()
    place_weights(peer_kernel, sources)

    step_lanes = min(256, sources)
    tiles = sources // step_lanes

    def compute(slot):
        values = []
        for chunk in range(chunks):
            code = blocks[slot, chunk]
            at_scale = local * main + rest
            scale = code[:, at_scale : at_scale + 1].astype(F32) * (1.0 / CODE_TOP)
            values.append(decode(code, scale))
        high, low = split(jnp.concatenate(values, axis=0))
        tail = local * main
        for j in range(local):
            left = jnp.concatenate(
                [
                    high[:, j * main : (j + 1) * main],
                    low[:, j * main : (j + 1) * main],
                    high[:, tail : tail + LANES],
                    low[:, tail : tail + LANES],
                ],
                axis=1,
            )
            for half in range(2):
                for tile in range(tiles):
                    lanes = slice(tile * step_lanes, (tile + 1) * step_lanes)
                    first = half * sources + tile * step_lanes
                    source = jnp.dot(
                        left,
                        weights[j, :, first : first + step_lanes],
                        preferred_element_type=F32,
                    )
                    real = source[:span]
                    imag = source[span:]
                    magnitude = real * real + imag * imag
                    inverse = lax.rsqrt(magnitude + PHASE_FLOOR)
                    acc[half, 0, :, lanes] += magnitude
                    acc[half, 1, :, lanes] += real * inverse
                    acc[half, 2, :, lanes] += imag * inverse

    def arrived(slot, chunk):
        pltpu.make_async_remote_copy(
            src_ref=blocks.at[slot, chunk],
            dst_ref=blocks.at[slot, chunk],
            send_sem=pair_send.at[0],
            recv_sem=recv.at[slot, chunk],
            device_id={"trial": partner},
            device_id_type=MESH,
        ).wait_recv()

    def event(e, carry):
        ka = e // inner
        kb = e % inner
        oa = nearest(ka, a, outer)
        ob = nearest(kb, b, inner)

        @pl.when(kb > 0)
        def _():
            for chunk in range(chunks):
                arrived(oa * inner + ob, chunk)
                inner_sends(oa, ob, chunk, start)

        compute(oa * inner + ob)

        @pl.when((kb == 0) & (ka + 1 < outer))
        def _():
            na = nearest(ka + 1, a, outer)
            for chunk in range(chunks):
                arrived(na * inner + b, chunk)
                outer_sends(na, chunk, start)
                inner_sends(na, b, chunk, start)

        return carry

    lax.fori_loop(0, outer * inner, event, 0)

    pair_copy = pltpu.make_async_remote_copy(
        src_ref=acc.at[1],
        dst_ref=peer_acc,
        send_sem=pair_send.at[1],
        recv_sem=pair_recv.at[1],
        device_id={"trial": partner},
        device_id_type=MESH,
    )
    pair_copy.start()
    for half in range(2):
        total = acc[half, 0, 0:8, :]
        for row in range(8, span, 8):
            total = total + acc[half, 0, row : row + 8, :]
        out_sums[half] = total
    sum_copies = []
    for index, (step, flip) in enumerate(others):
        slot = step * 2 + flip
        sum_copies.append(
            pltpu.make_async_remote_copy(
                src_ref=out_sums.at[flip],
                dst_ref=sums.at[slot - 1],
                send_sem=sum_send.at[index],
                recv_sem=sum_recv.at[index],
                device_id=other(step, flip),
                device_id_type=MESH,
            )
        )
    for copy in sum_copies:
        copy.start()

    trials = outer * inner * 2 * local
    pair_copy.wait()
    real = acc[0, 1] + peer_acc[1]
    imag = acc[0, 2] + peer_acc[2]
    itc_ref[...] = real * real + imag * imag
    rel_ref[...] = (acc[0, 0] + peer_acc[0]) / trials
    total = out_sums[0]
    for index, copy in enumerate(sum_copies):
        copy.wait()
        total = total + sums[index]
    mean_ref[...] = jnp.sum(total, axis=0, keepdims=True) / trials / (span * groups)

    def drain(e, carry):
        oa = e // inner
        ob = e % inner
        for chunk in range(chunks):
            inner_sends(oa, ob, chunk, finish)

            @pl.when(ob == b)
            def _():
                outer_sends(oa, chunk, finish)

        return carry

    lax.fori_loop(0, outer * inner, drain, 0)


def shards(signals, kernel, freqs):
    local, chans, samples = signals.shape
    sources = kernel.shape[0]
    span = freqs.shape[0] * TOUT
    groups = lax.axis_size("freq")
    chips = lax.axis_size("trial") // 2
    outer, inner = grid_of(chips)
    main = chans // LANES * LANES
    width = local * main + LANES
    depth = 2 * (main + LANES)
    chunks = 2
    vmem = pl.BlockSpec(memory_space=pltpu.VMEM)
    out = jax.ShapeDtypeStruct((span, sources), F32)
    dma = pltpu.SemaphoreType.DMA
    power, phase, mean_power = pl.pallas_call(
        functools.partial(body, outer, inner, groups),
        out_shape=(out, out, jax.ShapeDtypeStruct((1, sources), F32)),
        in_specs=[pl.BlockSpec(memory_space=pltpu.SMEM), vmem, vmem],
        out_specs=(vmem, vmem, vmem),
        scratch_shapes=[
            pltpu.VMEM((4 * span, samples), BF16),
            pltpu.VMEM((2 * span, width), F32),
            pltpu.VMEM((LANES, samples), BF16),
            pltpu.VMEM((chips, chunks, span, width), BF16),
            pltpu.VMEM((chans, sources), BF16),
            pltpu.VMEM((LANES // local, sources), BF16),
            pltpu.VMEM((local, depth, 2 * sources), BF16),
            pltpu.VMEM((2, 3, span, sources), F32),
            pltpu.VMEM((3, span, sources), F32),
            pltpu.VMEM((2 * groups - 1, 8, sources), F32),
            pltpu.VMEM((2, 8, sources), F32),
            dma((chips, chunks)),
            dma((2, outer, chunks)),
            dma((2, chips, chunks)),
            dma((2,)),
            dma((2,)),
            dma((2 * groups - 1,)),
            dma((2 * groups - 1,)),
        ],
        compiler_params=pltpu.CompilerParams(collective_id=0, has_side_effects=True),
    )(freqs, signals, kernel.T)
    rel_power = power / (mean_power + MEAN_EPSILON)
    itc_score = phase / (chips * 2 * local)
    return rel_power.T, itc_score.T


def solution(mesh):
    return jax.shard_map(
        shards,
        mesh=mesh,
        in_specs=(P("trial", None, None), P("trial", None), P("freq")),
        out_specs=(P("trial", "freq"), P("trial", "freq")),
        check_vma=False,
    )
```

```python
import functools
import math

import jax
import jax.numpy as jnp
from jax import lax
from jax.experimental import pallas as pl
from jax.experimental.pallas import tpu as pltpu
from jax.sharding import PartitionSpec as P

TOUT = 16
CYCLES = 7.0
SAMPLE_RATE = 1000.0
PHASE_FLOOR = 0.25
MEAN_EPSILON = 1e-06
LANES = 128
MESH = pl.DeviceIdType.MESH
F32 = jnp.float32
BF16 = jnp.bfloat16


def grid_of(chips):
    outer = 1
    while outer * outer < chips or chips % outer:
        outer += 1
    return outer, chips // outer


def polynomial(x2, terms):
    total = jnp.full_like(x2, terms[-1])
    for term in reversed(terms[:-1]):
        total = total * x2 + term
    return total


SIN_TERMS = [(-1) ** i * math.pi ** (2 * i + 1) / math.factorial(2 * i + 1) for i in range(8)]
COS_TERMS = [(-1) ** i * math.pi ** (2 * i) / math.factorial(2 * i) for i in range(8)]


def wavelet_rows(freq, points, samples):
    stride = samples // points
    moments = lax.broadcasted_iota(jnp.int32, (points, samples), 1)
    centres = lax.broadcasted_iota(jnp.int32, (points, samples), 0) * stride + stride // 2
    scaled = (moments - centres).astype(F32) * freq
    rate = 2.0 * math.pi / (CYCLES * SAMPLE_RATE)
    envelope = jnp.exp(scaled * scaled * (-0.5 * rate * rate)) * (freq * (8.0 * rate))
    turns = scaled * (1.0 / SAMPLE_RATE)
    part = turns - jnp.floor(turns + 0.5)
    square = part * part
    half_sin = part * polynomial(square, SIN_TERMS)
    half_cos = polynomial(square, COS_TERMS)
    return (
        envelope * (1.0 - 2.0 * half_sin * half_sin),
        envelope * (2.0 * half_sin * half_cos),
    )


def row_parts(rows):
    unit = 16
    crossed = rows // 5 // unit * unit
    rest = rows - crossed
    half = -(-rest // 2 // unit) * unit
    return ((0, crossed, True), (crossed, half, False), (crossed + half, rest - half, False))


def split(x):
    high = x.astype(BF16)
    return high, (x - high.astype(F32)).astype(BF16)


POWER_LOG = 4
CODE_TOP = 2.0 ** (125.0 / 2**POWER_LOG)


def encode(rows, inverse):
    x = rows * inverse
    y = x * x
    for _ in range(POWER_LOG - 1):
        y = y * y
    return jnp.where(x < 0, -y, y).astype(BF16)


def decode(code, scale):
    y = code.astype(F32)
    size = jnp.maximum(jnp.abs(y), 1.2e-38)
    x = jnp.exp(jnp.log(size) * (1.0 / 2**POWER_LOG)) * scale
    return jnp.where(y < 0, -x, jnp.where(y > 0, x, 0.0))


def body(
    outer,
    inner,
    groups,
    freqs_ref,
    signals_hbm,
    kernel_hbm,
    rel_ref,
    itc_ref,
    mean_ref,
    signals_ref,
    kernel_ref,
    load_sem,
    table,
    plain,
    rest_rows,
    blocks,
    peer_kernel,
    rest_pad,
    weights,
    acc,
    peer_acc,
    sums,
    out_sums,
    recv,
    outer_send,
    inner_send,
    pair_send,
    pair_recv,
    sum_send,
    sum_recv,
):
    signals_load = pltpu.make_async_copy(signals_hbm, signals_ref, load_sem.at[0])
    signals_load.start()
    kernel_load = pltpu.make_async_copy(kernel_hbm, kernel_ref, load_sem.at[1])
    kernel_load.start()
    local, chans, samples = signals_ref.shape
    sources = kernel_ref.shape[1]
    bands = freqs_ref.shape[0]
    span = bands * TOUT
    main = chans // LANES * LANES
    rest = chans - main
    slot_rows = LANES // local
    parts = row_parts(2 * span)
    chunks = len(parts)

    group = lax.axis_index("freq")
    place = lax.axis_index("trial")
    core = place % 2
    chip = place // 2
    a = chip // inner
    b = chip % inner
    partner = place + 1 - 2 * core

    def at(oa, ob):
        return (oa * inner + ob) * 2 + core

    barrier = pltpu.get_barrier_semaphore()

    def greet(target):
        pl.semaphore_signal(barrier, inc=1, device_id=target, device_id_type=MESH)

    for ahead in (-1, 1):
        ia = a + ahead
        ib = b + ahead

        @pl.when((ia >= 0) & (ia < outer))
        def _():
            greet({"trial": at(ia, b)})

        @pl.when((ib >= 0) & (ib < inner))
        def _():
            greet({"trial": at(a, ib)})

    others = []
    for step in range(groups):
        for flip in range(2):
            if step or flip:
                others.append((step, flip))

    def other(step, flip):
        there = (group + step) % groups
        seat = partner if flip else place
        return {"freq": there, "trial": seat}

    for step, flip in others:
        greet(other(step, flip))
    near = (
        jnp.minimum(a, 1)
        + jnp.minimum(outer - 1 - a, 1)
        + jnp.minimum(b, 1)
        + jnp.minimum(inner - 1 - b, 1)
    )
    pl.semaphore_wait(barrier, near + len(others))

    kernel_copy = pltpu.make_async_remote_copy(
        src_ref=kernel_hbm,
        dst_ref=peer_kernel,
        send_sem=pair_send.at[0],
        recv_sem=pair_recv.at[0],
        device_id={"trial": partner},
        device_id_type=MESH,
    )
    kernel_copy.start()

    for band in range(bands):
        cos_rows, sin_rows = wavelet_rows(freqs_ref[band], TOUT, samples)
        for half, rows in enumerate((cos_rows, sin_rows)):
            high, low = split(rows)
            first = half * span + band * TOUT
            table[first : first + TOUT, :] = high
            table[2 * span + first : 2 * span + first + TOUT, :] = low
    rest_rows[...] = jnp.zeros_like(rest_rows)
    signals_load.wait()
    for j in range(local):
        rest_rows[j * slot_rows : j * slot_rows + rest, :] = signals_ref[j, main:chans, :]

    mine = a * inner + b
    pieces = [(j * main, main, functools.partial(lambda j: signals_ref[j, 0:main, :], j)) for j in range(local)]
    pieces.append((local * main, LANES, lambda: rest_rows[...]))
    top = jnp.zeros((2 * span, 1), F32)
    for start, width, load in pieces:
        both = lax.dot_general(
            table[...], load(), (((1,), (1,)), ((), ())), preferred_element_type=F32
        )
        value = both[: 2 * span] + both[2 * span :]
        plain[:, start : start + width] = value
        top = jnp.maximum(top, jnp.max(jnp.abs(value), axis=1, keepdims=True))
    scale = jnp.maximum(top * 1.01, 1e-30).astype(BF16)
    inverse = CODE_TOP / scale.astype(F32)
    def neighbour_copy(slot, chunk, sems, ahead, target):
        first, count, _ = parts[chunk]
        rows = pl.ds(first, count)
        return pltpu.make_async_remote_copy(
            src_ref=blocks.at[slot, rows],
            dst_ref=blocks.at[slot, rows],
            send_sem=sems.at[(ahead + 1) // 2, slot, chunk],
            recv_sem=recv.at[slot, chunk],
            device_id={"trial": target},
            device_id_type=MESH,
        )

    def sends(oa, ob, chunk, act):
        slot = oa * inner + ob
        inner_first = parts[chunk][2]
        along_outer = (oa >= 0) if inner_first else (ob == b)
        along_inner = (oa == a) if inner_first else (oa >= 0)

        @pl.when(along_outer & (oa <= a) & (a + 1 < outer))
        def _():
            act(neighbour_copy(slot, chunk, outer_send, 1, at(a + 1, b)))

        @pl.when(along_outer & (oa >= a) & (a >= 1))
        def _():
            act(neighbour_copy(slot, chunk, outer_send, -1, at(a - 1, b)))

        @pl.when(along_inner & (ob <= b) & (b + 1 < inner))
        def _():
            act(neighbour_copy(slot, chunk, inner_send, 1, at(a, b + 1)))

        @pl.when(along_inner & (ob >= b) & (b >= 1))
        def _():
            act(neighbour_copy(slot, chunk, inner_send, -1, at(a, b - 1)))

    def start(copy):
        copy.start()

    def finish(copy):
        copy.wait_send()

    def nearest(k, here, count):
        left = here
        right = count - 1 - here
        both = 2 * jnp.minimum(left, right)
        dist = jnp.where(k <= both, (k + 1) // 2, k - both // 2)
        to_left = jnp.where(k <= both, k % 2, jnp.where(left > right, 1, 0))
        return here + dist - 2 * dist * to_left

    for chunk, (first, count, _) in enumerate(parts):
        rows = slice(first, first + count)
        lane = lax.broadcasted_iota(jnp.int32, (count, LANES), 1)
        for at_lane, width, _ in pieces:
            coded = encode(plain[rows, at_lane : at_lane + width], inverse[rows])
            if at_lane == local * main:
                coded = jnp.where(lane == rest, scale[rows].astype(F32), coded.astype(F32)).astype(BF16)
            blocks[mine, rows, at_lane : at_lane + width] = coded
        sends(a, b, chunk, start)

    acc[...] = jnp.zeros_like(acc)

    def place_weights(ref, first):
        wide = ref[0:main, :]
        rest_pad[...] = jnp.zeros_like(rest_pad)
        rest_pad[0:rest, :] = ref[main:chans, :]
        tail = rest_pad[...]
        cols = slice(first, first + sources)
        for j in range(local):
            for copy in range(2):
                weights[j, copy * main : (copy + 1) * main, cols] = wide
                base = 2 * main + copy * LANES
                for other_slot in range(local):
                    rows = slice(base + other_slot * slot_rows, base + (other_slot + 1) * slot_rows)
                    weights[j, rows, cols] = tail if other_slot == j else jnp.zeros_like(tail)

    kernel_load.wait()
    place_weights(kernel_ref, 0)
    kernel_copy.wait()
    place_weights(peer_kernel, sources)

    step_lanes = min(256, sources)
    tiles = sources // step_lanes

    pair_copy = pltpu.make_async_remote_copy(
        src_ref=acc.at[1],
        dst_ref=peer_acc,
        send_sem=pair_send.at[1],
        recv_sem=pair_recv.at[1],
        device_id={"trial": partner},
        device_id_type=MESH,
    )

    def compute(slot, last):
        code = blocks[slot]
        tail = local * main
        scale = code[:, tail + rest : tail + rest + 1].astype(F32) * (1.0 / CODE_TOP)
        high, low = split(decode(code, scale))
        lefts = []
        for j in range(local):
            left = jnp.concatenate(
                [
                    high[:, j * main : (j + 1) * main],
                    low[:, j * main : (j + 1) * main],
                    high[:, tail : tail + LANES],
                    low[:, tail : tail + LANES],
                ],
                axis=1,
            )
            lefts.append(left)
        for half in (1, 0):
            for j in range(local):
                for tile in range(tiles):
                    lanes = slice(tile * step_lanes, (tile + 1) * step_lanes)
                    first = half * sources + tile * step_lanes
                    source = jnp.dot(
                        lefts[j],
                        weights[j, :, first : first + step_lanes],
                        preferred_element_type=F32,
                    )
                    real = source[:span]
                    imag = source[span:]
                    magnitude = real * real + imag * imag
                    inverse = lax.rsqrt(magnitude + PHASE_FLOOR)
                    acc[half, 0, :, lanes] += magnitude
                    acc[half, 1, :, lanes] += real * inverse
                    acc[half, 2, :, lanes] += imag * inverse
            if half:

                @pl.when(last)
                def _():
                    pair_copy.start()

    def arrived(slot, chunk):
        first, count, _ = parts[chunk]
        rows = pl.ds(first, count)
        pltpu.make_async_remote_copy(
            src_ref=blocks.at[slot, rows],
            dst_ref=blocks.at[slot, rows],
            send_sem=pair_send.at[0],
            recv_sem=recv.at[slot, chunk],
            device_id={"trial": partner},
            device_id_type=MESH,
        ).wait_recv()

    def event(e, carry):
        ka = e // inner
        kb = e % inner
        oa = nearest(ka, a, outer)
        ob = nearest(kb, b, inner)

        @pl.when(kb > 0)
        def _():
            for chunk in range(chunks):
                arrived(oa * inner + ob, chunk)
                sends(oa, ob, chunk, start)

        compute(oa * inner + ob, e == outer * inner - 1)

        @pl.when((kb == 0) & (ka + 1 < outer))
        def _():
            na = nearest(ka + 1, a, outer)
            for chunk in range(chunks):
                arrived(na * inner + b, chunk)
                sends(na, b, chunk, start)

        return carry

    lax.fori_loop(0, outer * inner, event, 0)

    for half in range(2):
        total = acc[half, 0, 0:8, :]
        for row in range(8, span, 8):
            total = total + acc[half, 0, row : row + 8, :]
        out_sums[half] = total
    sum_copies = []
    for index, (step, flip) in enumerate(others):
        slot = step * 2 + flip
        sum_copies.append(
            pltpu.make_async_remote_copy(
                src_ref=out_sums.at[flip],
                dst_ref=sums.at[slot - 1],
                send_sem=sum_send.at[index],
                recv_sem=sum_recv.at[index],
                device_id=other(step, flip),
                device_id_type=MESH,
            )
        )
    for copy in sum_copies:
        copy.start()

    trials = outer * inner * 2 * local
    pair_copy.wait()
    real = acc[0, 1] + peer_acc[1]
    imag = acc[0, 2] + peer_acc[2]
    itc_ref[...] = real * real + imag * imag
    rel_ref[...] = (acc[0, 0] + peer_acc[0]) / trials
    total = out_sums[0]
    for index, copy in enumerate(sum_copies):
        copy.wait()
        total = total + sums[index]
    mean_power = jnp.sum(total, axis=0, keepdims=True) / trials / (span * groups)
    mean_ref[...] = mean_power + MEAN_EPSILON

    def drain(e, carry):
        oa = e // inner
        ob = e % inner
        for chunk in range(chunks):
            sends(oa, ob, chunk, finish)

        return carry

    lax.fori_loop(0, outer * inner, drain, 0)


def shards(signals, kernel, freqs):
    local, chans, samples = signals.shape
    sources = kernel.shape[0]
    span = freqs.shape[0] * TOUT
    groups = lax.axis_size("freq")
    chips = lax.axis_size("trial") // 2
    outer, inner = grid_of(chips)
    main = chans // LANES * LANES
    width = local * main + LANES
    depth = 2 * (main + LANES)
    chunks = len(row_parts(2 * span))
    hbm = pl.BlockSpec(memory_space=pl.ANY)
    vmem = pl.BlockSpec(memory_space=pltpu.VMEM)
    out = jax.ShapeDtypeStruct((span, sources), F32)
    dma = pltpu.SemaphoreType.DMA
    power, phase, mean_power = pl.pallas_call(
        functools.partial(body, outer, inner, groups),
        out_shape=(out, out, jax.ShapeDtypeStruct((1, sources), F32)),
        in_specs=[pl.BlockSpec(memory_space=pltpu.SMEM), hbm, hbm],
        out_specs=(vmem, vmem, vmem),
        scratch_shapes=[
            pltpu.VMEM((local, chans, samples), BF16),
            pltpu.VMEM((chans, sources), BF16),
            dma((2,)),
            pltpu.VMEM((4 * span, samples), BF16),
            pltpu.VMEM((2 * span, width), F32),
            pltpu.VMEM((LANES, samples), BF16),
            pltpu.VMEM((chips, 2 * span, width), BF16),
            pltpu.VMEM((chans, sources), BF16),
            pltpu.VMEM((LANES // local, sources), BF16),
            pltpu.VMEM((local, depth, 2 * sources), BF16),
            pltpu.VMEM((2, 3, span, sources), F32),
            pltpu.VMEM((3, span, sources), F32),
            pltpu.VMEM((2 * groups - 1, 8, sources), F32),
            pltpu.VMEM((2, 8, sources), F32),
            dma((chips, chunks)),
            dma((2, chips, chunks)),
            dma((2, chips, chunks)),
            dma((2,)),
            dma((2,)),
            dma((2 * groups - 1,)),
            dma((2 * groups - 1,)),
        ],
        compiler_params=pltpu.CompilerParams(collective_id=0, has_side_effects=True),
    )(freqs, signals, kernel.T)
    rel_power = power / mean_power
    itc_score = phase / (chips * 2 * local)
    return rel_power.T, itc_score.T


def solution(mesh):
    return jax.shard_map(
        shards,
        mesh=mesh,
        in_specs=(P("trial", None, None), P("trial", None), P("freq")),
        out_specs=(P("trial", "freq"), P("trial", "freq")),
        check_vma=False,
    )
```

```python
import functools
import math

import jax
import jax.numpy as jnp
from jax import lax
from jax.experimental import pallas as pl
from jax.experimental.pallas import tpu as pltpu
from jax.sharding import PartitionSpec as P

TOUT = 16
CYCLES = 7.0
SAMPLE_RATE = 1000.0
PHASE_FLOOR = 0.25
MEAN_EPSILON = 1e-06
LANES = 128
MESH = pl.DeviceIdType.MESH
F32 = jnp.float32
BF16 = jnp.bfloat16


def grid_of(chips):
    outer = 1
    while outer * outer < chips or chips % outer:
        outer += 1
    return outer, chips // outer


def polynomial(x2, terms):
    total = jnp.full_like(x2, terms[-1])
    for term in reversed(terms[:-1]):
        total = total * x2 + term
    return total


SIN_TERMS = [(-1) ** i * math.pi ** (2 * i + 1) / math.factorial(2 * i + 1) for i in range(8)]
COS_TERMS = [(-1) ** i * math.pi ** (2 * i) / math.factorial(2 * i) for i in range(8)]


def wavelet_rows(freq, points, samples):
    stride = samples // points
    moments = lax.broadcasted_iota(jnp.int32, (points, samples), 1)
    centres = lax.broadcasted_iota(jnp.int32, (points, samples), 0) * stride + stride // 2
    scaled = (moments - centres).astype(F32) * freq
    rate = 2.0 * math.pi / (CYCLES * SAMPLE_RATE)
    envelope = jnp.exp(scaled * scaled * (-0.5 * rate * rate)) * (freq * (8.0 * rate))
    turns = scaled * (1.0 / SAMPLE_RATE)
    part = turns - jnp.floor(turns + 0.5)
    square = part * part
    half_sin = part * polynomial(square, SIN_TERMS)
    half_cos = polynomial(square, COS_TERMS)
    return (
        envelope * (1.0 - 2.0 * half_sin * half_sin),
        envelope * (2.0 * half_sin * half_cos),
    )


def row_parts(rows):
    unit = 16
    half = rows // 2 // unit * unit
    return ((0, half, False), (half, rows - half, False))


def split(x):
    high = x.astype(BF16)
    return high, (x - high.astype(F32)).astype(BF16)


POWER_LOG = 4
CODE_TOP = 2.0 ** (125.0 / 2**POWER_LOG)


def encode(rows, inverse):
    x = rows * inverse
    y = x * x
    for _ in range(POWER_LOG - 1):
        y = y * y
    return jnp.where(x < 0, -y, y).astype(BF16)


def decode(code, scale):
    y = code.astype(F32)
    size = jnp.maximum(jnp.abs(y), 1.2e-38)
    x = jnp.exp(jnp.log(size) * (1.0 / 2**POWER_LOG)) * scale
    return jnp.where(y < 0, -x, jnp.where(y > 0, x, 0.0))


def body(
    outer,
    inner,
    groups,
    freqs_ref,
    signals_hbm,
    kernel_hbm,
    rel_ref,
    itc_ref,
    mean_ref,
    signals_ref,
    kernel_ref,
    load_sem,
    table,
    plain,
    rest_rows,
    blocks,
    peer_kernel,
    rest_pad,
    weights,
    acc,
    peer_acc,
    sums,
    out_sums,
    recv,
    outer_send,
    inner_send,
    pair_send,
    pair_recv,
    sum_send,
    sum_recv,
):
    signals_load = pltpu.make_async_copy(signals_hbm, signals_ref, load_sem.at[0])
    signals_load.start()
    kernel_load = pltpu.make_async_copy(kernel_hbm, kernel_ref, load_sem.at[1])
    kernel_load.start()
    local, chans, samples = signals_ref.shape
    sources = kernel_ref.shape[1]
    bands = freqs_ref.shape[0]
    span = bands * TOUT
    main = chans // LANES * LANES
    rest = chans - main
    slot_rows = LANES // local
    parts = row_parts(2 * span)
    chunks = len(parts)

    group = lax.axis_index("freq")
    place = lax.axis_index("trial")
    core = place % 2
    chip = place // 2
    a = chip // inner
    b = chip % inner
    partner = place + 1 - 2 * core

    def at(oa, ob):
        return (oa * inner + ob) * 2 + core

    barrier = pltpu.get_barrier_semaphore()

    def greet(target):
        pl.semaphore_signal(barrier, inc=1, device_id=target, device_id_type=MESH)

    for ahead in (-1, 1):
        ia = a + ahead
        ib = b + ahead

        @pl.when((ia >= 0) & (ia < outer))
        def _():
            greet({"trial": at(ia, b)})

        @pl.when((ib >= 0) & (ib < inner))
        def _():
            greet({"trial": at(a, ib)})

    others = []
    for step in range(groups):
        for flip in range(2):
            if step or flip:
                others.append((step, flip))

    def other(step, flip):
        there = (group + step) % groups
        seat = partner if flip else place
        return {"freq": there, "trial": seat}

    for step, flip in others:
        greet(other(step, flip))
    near = (
        jnp.minimum(a, 1)
        + jnp.minimum(outer - 1 - a, 1)
        + jnp.minimum(b, 1)
        + jnp.minimum(inner - 1 - b, 1)
    )
    pl.semaphore_wait(barrier, near + len(others))

    kernel_copy = pltpu.make_async_remote_copy(
        src_ref=kernel_hbm,
        dst_ref=peer_kernel,
        send_sem=pair_send.at[0],
        recv_sem=pair_recv.at[0],
        device_id={"trial": partner},
        device_id_type=MESH,
    )
    kernel_copy.start()

    for band in range(bands):
        cos_rows, sin_rows = wavelet_rows(freqs_ref[band], TOUT, samples)
        for half, rows in enumerate((cos_rows, sin_rows)):
            high, low = split(rows)
            first = half * span + band * TOUT
            table[first : first + TOUT, :] = high
            table[2 * span + first : 2 * span + first + TOUT, :] = low
    rest_rows[...] = jnp.zeros_like(rest_rows)
    signals_load.wait()
    for j in range(local):
        rest_rows[j * slot_rows : j * slot_rows + rest, :] = signals_ref[j, main:chans, :]

    mine = a * inner + b
    pieces = [(j * main, main, functools.partial(lambda j: signals_ref[j, 0:main, :], j)) for j in range(local)]
    pieces.append((local * main, LANES, lambda: rest_rows[...]))
    top = jnp.zeros((2 * span, 1), F32)
    for start, width, load in pieces:
        both = lax.dot_general(
            table[...], load(), (((1,), (1,)), ((), ())), preferred_element_type=F32
        )
        value = both[: 2 * span] + both[2 * span :]
        plain[:, start : start + width] = value
        top = jnp.maximum(top, jnp.max(jnp.abs(value), axis=1, keepdims=True))
    scale = jnp.maximum(top * 1.01, 1e-30).astype(BF16)
    inverse = CODE_TOP / scale.astype(F32)
    def neighbour_copy(slot, chunk, sems, ahead, target):
        first, count, _ = parts[chunk]
        rows = pl.ds(first, count)
        return pltpu.make_async_remote_copy(
            src_ref=blocks.at[slot, rows],
            dst_ref=blocks.at[slot, rows],
            send_sem=sems.at[(ahead + 1) // 2, slot, chunk],
            recv_sem=recv.at[slot, chunk],
            device_id={"trial": target},
            device_id_type=MESH,
        )

    def sends(oa, ob, chunk, act):
        slot = oa * inner + ob
        inner_first = parts[chunk][2]
        along_outer = (oa >= 0) if inner_first else (ob == b)
        along_inner = (oa == a) if inner_first else (oa >= 0)

        @pl.when(along_outer & (oa <= a) & (a + 1 < outer))
        def _():
            act(neighbour_copy(slot, chunk, outer_send, 1, at(a + 1, b)))

        @pl.when(along_outer & (oa >= a) & (a >= 1))
        def _():
            act(neighbour_copy(slot, chunk, outer_send, -1, at(a - 1, b)))

        @pl.when(along_inner & (ob <= b) & (b + 1 < inner))
        def _():
            act(neighbour_copy(slot, chunk, inner_send, 1, at(a, b + 1)))

        @pl.when(along_inner & (ob >= b) & (b >= 1))
        def _():
            act(neighbour_copy(slot, chunk, inner_send, -1, at(a, b - 1)))

    def start(copy):
        copy.start()

    def finish(copy):
        copy.wait_send()

    def nearest(k, here, count):
        left = here
        right = count - 1 - here
        both = 2 * jnp.minimum(left, right)
        dist = jnp.where(k <= both, (k + 1) // 2, k - both // 2)
        to_left = jnp.where(k <= both, k % 2, jnp.where(left > right, 1, 0))
        return here + dist - 2 * dist * to_left

    for chunk, (first, count, _) in enumerate(parts):
        rows = slice(first, first + count)
        lane = lax.broadcasted_iota(jnp.int32, (count, LANES), 1)
        for at_lane, width, _ in pieces:
            coded = encode(plain[rows, at_lane : at_lane + width], inverse[rows])
            if at_lane == local * main:
                coded = jnp.where(lane == rest, scale[rows].astype(F32), coded.astype(F32)).astype(BF16)
            blocks[mine, rows, at_lane : at_lane + width] = coded
        sends(a, b, chunk, start)

    acc[...] = jnp.zeros_like(acc)

    def place_weights(ref, first):
        wide = ref[0:main, :]
        rest_pad[...] = jnp.zeros_like(rest_pad)
        rest_pad[0:rest, :] = ref[main:chans, :]
        tail = rest_pad[...]
        cols = slice(first, first + sources)
        for j in range(local):
            for copy in range(2):
                weights[j, copy * main : (copy + 1) * main, cols] = wide
                base = 2 * main + copy * LANES
                for other_slot in range(local):
                    rows = slice(base + other_slot * slot_rows, base + (other_slot + 1) * slot_rows)
                    weights[j, rows, cols] = tail if other_slot == j else jnp.zeros_like(tail)

    kernel_load.wait()
    place_weights(kernel_ref, 0)
    kernel_copy.wait()
    place_weights(peer_kernel, sources)

    step_lanes = min(256, sources)
    tiles = sources // step_lanes

    pair_copy = pltpu.make_async_remote_copy(
        src_ref=acc.at[1],
        dst_ref=peer_acc,
        send_sem=pair_send.at[1],
        recv_sem=pair_recv.at[1],
        device_id={"trial": partner},
        device_id_type=MESH,
    )

    def compute(slot, last):
        code = blocks[slot]
        tail = local * main
        scale = code[:, tail + rest : tail + rest + 1].astype(F32) * (1.0 / CODE_TOP)
        high, low = split(decode(code, scale))
        lefts = []
        for j in range(local):
            left = jnp.concatenate(
                [
                    high[:, j * main : (j + 1) * main],
                    low[:, j * main : (j + 1) * main],
                    high[:, tail : tail + LANES],
                    low[:, tail : tail + LANES],
                ],
                axis=1,
            )
            lefts.append(left)
        for half in (1, 0):
            for j in range(local):
                for tile in range(tiles):
                    lanes = slice(tile * step_lanes, (tile + 1) * step_lanes)
                    first = half * sources + tile * step_lanes
                    source = jnp.dot(
                        lefts[j],
                        weights[j, :, first : first + step_lanes],
                        preferred_element_type=F32,
                    )
                    real = source[:span]
                    imag = source[span:]
                    magnitude = real * real + imag * imag
                    inverse = lax.rsqrt(magnitude + PHASE_FLOOR)
                    acc[half, 0, :, lanes] += magnitude
                    acc[half, 1, :, lanes] += real * inverse
                    acc[half, 2, :, lanes] += imag * inverse
            if half:

                @pl.when(last)
                def _():
                    pair_copy.start()

    def arrived(slot, chunk):
        first, count, _ = parts[chunk]
        rows = pl.ds(first, count)
        pltpu.make_async_remote_copy(
            src_ref=blocks.at[slot, rows],
            dst_ref=blocks.at[slot, rows],
            send_sem=pair_send.at[0],
            recv_sem=recv.at[slot, chunk],
            device_id={"trial": partner},
            device_id_type=MESH,
        ).wait_recv()

    reach = jnp.maximum(a, outer - 1 - a)
    last_side = jnp.where((outer - 1 - a == reach) & (reach > 0), 1, 0)

    def origin(dist, side):
        there = a - dist + 2 * dist * side
        exists = (there >= 0) & (there < outer) & ((dist > 0) | (side == 0))
        return there, exists

    def event(e, carry):
        dist = e // (2 * inner)
        kb = e % (2 * inner) // 2
        side = e % 2
        oa, exists = origin(dist, side)
        ob = nearest(kb, b, inner)

        @pl.when(exists)
        def _():
            @pl.when(kb > 0)
            def _():
                for chunk in range(chunks):
                    arrived(oa * inner + ob, chunk)
                    sends(oa, ob, chunk, start)

            last = (dist == reach) & (kb == inner - 1) & (side == last_side)
            compute(oa * inner + ob, last)

        @pl.when((kb == 0) & (side == 1))
        def _():
            for chunk in range(chunks):
                for next_side in range(2):
                    na, more = origin(dist + 1, next_side)

                    @pl.when(more)
                    def _():
                        arrived(na * inner + b, chunk)
                        sends(na, b, chunk, start)

        return carry

    lax.fori_loop(0, outer * inner * 2, event, 0)

    for half in range(2):
        total = acc[half, 0, 0:8, :]
        for row in range(8, span, 8):
            total = total + acc[half, 0, row : row + 8, :]
        out_sums[half] = total
    sum_copies = []
    for index, (step, flip) in enumerate(others):
        slot = step * 2 + flip
        sum_copies.append(
            pltpu.make_async_remote_copy(
                src_ref=out_sums.at[flip],
                dst_ref=sums.at[slot - 1],
                send_sem=sum_send.at[index],
                recv_sem=sum_recv.at[index],
                device_id=other(step, flip),
                device_id_type=MESH,
            )
        )
    for copy in sum_copies:
        copy.start()

    trials = outer * inner * 2 * local
    pair_copy.wait()
    real = acc[0, 1] + peer_acc[1]
    imag = acc[0, 2] + peer_acc[2]
    itc_ref[...] = real * real + imag * imag
    rel_ref[...] = (acc[0, 0] + peer_acc[0]) / trials
    total = out_sums[0]
    for index, copy in enumerate(sum_copies):
        copy.wait()
        total = total + sums[index]
    mean_power = jnp.sum(total, axis=0, keepdims=True) / trials / (span * groups)
    mean_ref[...] = mean_power + MEAN_EPSILON

    def drain(e, carry):
        oa = e // inner
        ob = e % inner
        for chunk in range(chunks):
            sends(oa, ob, chunk, finish)

        return carry

    lax.fori_loop(0, outer * inner, drain, 0)


def shards(signals, kernel, freqs):
    local, chans, samples = signals.shape
    sources = kernel.shape[0]
    span = freqs.shape[0] * TOUT
    groups = lax.axis_size("freq")
    chips = lax.axis_size("trial") // 2
    outer, inner = grid_of(chips)
    main = chans // LANES * LANES
    width = local * main + LANES
    depth = 2 * (main + LANES)
    chunks = len(row_parts(2 * span))
    hbm = pl.BlockSpec(memory_space=pl.ANY)
    vmem = pl.BlockSpec(memory_space=pltpu.VMEM)
    out = jax.ShapeDtypeStruct((span, sources), F32)
    dma = pltpu.SemaphoreType.DMA
    power, phase, mean_power = pl.pallas_call(
        functools.partial(body, outer, inner, groups),
        out_shape=(out, out, jax.ShapeDtypeStruct((1, sources), F32)),
        in_specs=[pl.BlockSpec(memory_space=pltpu.SMEM), hbm, hbm],
        out_specs=(vmem, vmem, vmem),
        scratch_shapes=[
            pltpu.VMEM((local, chans, samples), BF16),
            pltpu.VMEM((chans, sources), BF16),
            dma((2,)),
            pltpu.VMEM((4 * span, samples), BF16),
            pltpu.VMEM((2 * span, width), F32),
            pltpu.VMEM((LANES, samples), BF16),
            pltpu.VMEM((chips, 2 * span, width), BF16),
            pltpu.VMEM((chans, sources), BF16),
            pltpu.VMEM((LANES // local, sources), BF16),
            pltpu.VMEM((local, depth, 2 * sources), BF16),
            pltpu.VMEM((2, 3, span, sources), F32),
            pltpu.VMEM((3, span, sources), F32),
            pltpu.VMEM((2 * groups - 1, 8, sources), F32),
            pltpu.VMEM((2, 8, sources), F32),
            dma((chips, chunks)),
            dma((2, chips, chunks)),
            dma((2, chips, chunks)),
            dma((2,)),
            dma((2,)),
            dma((2 * groups - 1,)),
            dma((2 * groups - 1,)),
        ],
        compiler_params=pltpu.CompilerParams(collective_id=0, has_side_effects=True),
    )(freqs, signals, kernel.T)
    rel_power = power / mean_power
    itc_score = phase / (chips * 2 * local)
    return rel_power.T, itc_score.T


def solution(mesh):
    return jax.shard_map(
        shards,
        mesh=mesh,
        in_specs=(P("trial", None, None), P("trial", None), P("freq")),
        out_specs=(P("trial", "freq"), P("trial", "freq")),
        check_vma=False,
    )
```
